512 devices in a mesh: group: 16 (over y, z_hi), seq: 32 (over x, z_lo, core).
Axes of the slice: x: 4, y: 4, z: 16 (z_hi: 4, z_lo: 4; z = z_hi * 4 + z_lo), core: 2. Of those that a mesh axis runs over, the one named last changes fastest.
Arguments:
- features: bfloat16 [65536, 768], P(('group', 'seq')), may hold values from -6 to 6
- tiles: bfloat16 [65536, 1024], P(('group', 'seq')), may hold values from -0.5 to 0.5
- tile_src: int32 [512, 8], P(('group', 'seq')), may hold values from 0 to 15
- tile_count: int32 [512], P(('group', 'seq')), may hold values from 1 to 8, as said below
- node_bucket: int32 [65536], P(('group', 'seq')), may hold values from 0 to 15
- w_qk: bfloat16 [768, 1536], replicated, may hold values from -0.3125 to 0.3125
- w_v: bfloat16 [768, 768], replicated, may hold values from -1.25 to 1.25
- bias_table: float32 [32, 256], replicated, may hold values from -2 to 300
Outputs:
- attended: bfloat16 [65536, 768], P(('group', 'seq'))
The draws below stay inside these ranges and needn't reach their ends.
Inputs may be any that keep to these rules, and one draw needn't show every extreme that they name: `tile_count`: some row block uses all 8 slots.
All inputs are finite; a program needn't handle non-finite values.
Results may differ from the reference program's by a relative error of at most 0.012.
Values may be sent and summed in bfloat16 or wider, within the bound.
A program may use at most 64 MiB of HBM per device.

```python
import math
import jax
import jax.numpy as jnp
from jax import lax

D = 768
H = 32
HD = 24
NB = 16
TILES = 8
NODE_DEV = 128
GROUPS = 16
NODES_G = 4096
BLOCKS = 512
NODES = 65536
N_SEQ = 32


def draw_tile_count(key, part):
    counts = jax.random.randint(jax.random.fold_in(key, 11), (BLOCKS,), 1, TILES + 1)
    full_block = jax.random.randint(jax.random.fold_in(key, 12), (), 0, BLOCKS)
    return jnp.where(jnp.arange(BLOCKS) == full_block, TILES, counts).astype(jnp.int32)


def draw_bias_table(key, part):
    table_now = jax.random.uniform(jax.random.fold_in(key, 21), (H, NB, NB), jnp.float32, -2.0, 2.0)
    return table_now.reshape(H, NB * NB)


def set_ends(result, own_key, low, high):
    extent = result.shape
    index_at = [jax.random.randint(jax.random.fold_in(own_key, axis), (), 0, extent[axis]) for axis in range(len(extent))]
    result = result.at[tuple(index_at)].set(low)
    longest = extent.index(max(extent))
    index_at[longest] = (index_at[longest] + 1) % extent[longest]
    return result.at[tuple(index_at)].set(high)


def block_levels(rng, extent, pieces, least, high):
    def one(dim, shards_of):
        draws = jax.random.uniform(jax.random.fold_in(jax.random.fold_in(rng, 6), dim), (shards_of,), jnp.float32, least / len(pieces), high / len(pieces))
        return jnp.repeat(jnp.exp(draws), extent[dim] // shards_of).reshape((-1,) + (1,) * (len(extent) - dim - 1))

    gain = one(*pieces[0])
    for cut in pieces[1:]:
        gain = gain * one(*cut)
    return gain


def gaussian(rng, shape, deviation, most, cuts=(), dtype=jnp.bfloat16):
    array = deviation * jax.random.normal(rng, shape, jnp.float32)
    if cuts:
        array = array * block_levels(rng, shape, cuts, -0.22, 0.18)
    return jnp.clip(array, -most, most).astype(dtype)


def setup_inputs(seed: int = 0) -> dict:
    keys = jax.random.split(jax.random.key(seed), 9)
    features = gaussian(keys[0], (NODES, D), 1.0, 6.0, ((0, 512),))
    tiles = gaussian(keys[1], (NODES, TILES * NODE_DEV), NODE_DEV ** -0.5, 0.5, ((0, 512),))
    tile_src = set_ends(jax.random.randint(keys[2], (BLOCKS, TILES), 0, GROUPS), jax.random.fold_in(keys[2], 1), 0, GROUPS - 1).astype(jnp.int32)
    tile_count = draw_tile_count(jax.random.fold_in(keys[8], 71), 0)
    node_bucket = set_ends(jax.random.randint(keys[4], (NODES,), 0, NB), jax.random.fold_in(keys[4], 1), 0, NB - 1).astype(jnp.int32)
    w_qk = gaussian(keys[5], (D, 2 * D), (D // 2) ** -0.5, 0.3125)
    w_v = gaussian(keys[6], (D, D), (D // 32) ** -0.5, 1.25)
    bias_table = draw_bias_table(jax.random.fold_in(keys[8], 71), 0)
    return dict(features=features, tiles=tiles, tile_src=tile_src, tile_count=tile_count, node_bucket=node_bucket, w_qk=w_qk, w_v=w_v, bias_table=bias_table)


def reference(features, tiles, tile_src, tile_count, node_bucket, w_qk, w_v, bias_table):
    blocks_all = features.reshape(BLOCKS, NODE_DEV, D)
    tile_blocks = tiles.reshape(BLOCKS, NODE_DEV, TILES, NODE_DEV)

    def aggregate_block(block_id):
        block_ids = (tile_src[block_id] * N_SEQ + block_id % N_SEQ).astype(jnp.int32)
        chosen = blocks_all[block_ids].astype(jnp.float32)
        live_mask = (jnp.arange(TILES) < tile_count[block_id]).astype(jnp.float32)
        tile_weights = tile_blocks[block_id].astype(jnp.float32) * live_mask[None, :, None]
        summed = jnp.einsum('rtc,tcd->rd', tile_weights, chosen, precision=lax.Precision.HIGHEST)
        return blocks_all[block_id].astype(jnp.float32) + summed
    aggregated = lax.map(aggregate_block, jnp.arange(BLOCKS)).reshape(NODES, D)
    mean_square = lax.optimization_barrier(jnp.mean(aggregated * aggregated, axis=-1, keepdims=True))
    normed = (aggregated * lax.rsqrt(mean_square + 1e-06)).astype(jnp.bfloat16)
    query_key = jnp.dot(normed, w_qk, preferred_element_type=jnp.float32).astype(jnp.bfloat16)
    values = jnp.dot(normed, w_v, preferred_element_type=jnp.float32).astype(jnp.bfloat16)
    queries = query_key[:, :D].reshape(GROUPS, NODES_G, H, HD)
    keys_all = query_key[:, D:].reshape(GROUPS, NODES_G, H, HD)
    values_all = values.reshape(GROUPS, NODES_G, H, HD)
    buckets = node_bucket.reshape(GROUPS, NODES_G)
    bias_cube = bias_table.reshape(H, NB, NB)
    scale = 1.0 / math.sqrt(HD)

    def group_attention(operands):
        group_q, group_k, group_v, group_b = operands

        def one_head(head_id):
            scores = jnp.dot(group_q[:, head_id, :], group_k[:, head_id, :].T, preferred_element_type=jnp.float32) * scale
            row_bias = bias_cube[head_id][group_b]
            scores = scores + row_bias[:, group_b]
            peak = lax.optimization_barrier(jnp.max(scores, axis=-1, keepdims=True))
            weights = jnp.exp(scores - peak)
            total_weight = lax.optimization_barrier(jnp.sum(weights, axis=-1, keepdims=True))
            mixed = jnp.dot(weights.astype(jnp.bfloat16), group_v[:, head_id, :], preferred_element_type=jnp.float32)
            return mixed / total_weight
        return lax.map(one_head, jnp.arange(H))
    heads_out = lax.map(group_attention, (queries, keys_all, values_all, buckets))
    return heads_out.transpose(0, 2, 1, 3).reshape(NODES, D).astype(jnp.bfloat16)
```

```python
import functools
import math

import jax
import jax.numpy as jnp
from jax import lax
from jax.experimental import pallas as pl
from jax.experimental.pallas import tpu as pltpu
from jax.sharding import PartitionSpec as P

D = 768
H = 32
HD = 24
NB = 16
TILES = 8
ROWS = 128
NG = 16
NS = 32
NODES_G = ROWS * NS
PIECE = 80
CHUNKS = 4
CROWS = ROWS // CHUNKS
QB = 256
KC = 1024
SCALE_LOG2 = math.log2(math.e) / math.sqrt(HD)
LOG2E = math.log2(math.e)
MESH = pl.DeviceIdType.MESH
F32 = jnp.float32
BF16 = jnp.bfloat16


def aggregate_kernel(
    x_ref, tiles_ref, src_ref, cnt_ref, bucket_ref, wqk_ref, wv_ref,
    out_ref,
    gath, tiles_v, wqk_v, wv_v, qkv_t, send_sem, recv_sem, local_sem,
):
    g = lax.axis_index("group")
    y = g // 4
    z = lax.rem(g, 4)

    def gid(yy, zz):
        return lax.rem(yy, 4) * 4 + lax.rem(zz, 4)

    zp, zm = gid(y, z + 1), gid(y, z + 3)
    yp, ym = gid(y + 1, z), gid(y + 3, z)

    barrier = pltpu.get_barrier_semaphore()
    for peer in (zp, zm, yp, ym):
        pl.semaphore_signal(barrier, inc=1, device_id={"group": peer}, device_id_type=MESH)

    own = pltpu.make_async_copy(x_ref, gath.at[g], local_sem.at[0])
    own.start()
    loads = [
        pltpu.make_async_copy(tiles_ref, tiles_v, local_sem.at[1]),
        pltpu.make_async_copy(wqk_ref, wqk_v, local_sem.at[2]),
        pltpu.make_async_copy(wv_ref, wv_v, local_sem.at[3]),
    ]
    for load in loads:
        load.start()
    pl.semaphore_wait(barrier, 4)

    sent = []

    def block(origin, c):
        return gath.at[origin, pl.ds(c * CROWS, CROWS), :]

    def send(source, origin, c, peer):
        copy = pltpu.make_async_remote_copy(
            src_ref=source,
            dst_ref=block(origin, c),
            send_sem=send_sem.at[len(sent)],
            recv_sem=recv_sem.at[origin, c],
            device_id={"group": peer},
            device_id_type=MESH,
        )
        copy.start()
        sent.append(copy)

    def forward(origin, c, peer):
        send(block(origin, c), origin, c, peer)

    def arrive(origin, c):
        pltpu.make_async_remote_copy(
            src_ref=block(origin, c),
            dst_ref=block(origin, c),
            send_sem=send_sem.at[0],
            recv_sem=recv_sem.at[origin, c],
            device_id={"group": zp},
            device_id_type=MESH,
        ).wait_recv()

    half = CHUNKS // 2
    order = [c for pair in zip(range(half), range(half, CHUNKS)) for c in pair]
    for c in order:
        for peer in (zp, zm):
            send(x_ref.at[pl.ds(c * CROWS, CROWS), :], g, c, peer)
    for c in order:
        for peer in (yp, ym):
            send(x_ref.at[pl.ds(c * CROWS, CROWS), :], g, c, peer)

    def second_y(zz, c):
        if c < half:
            arrive(gid(y + 3, zz), c)
            forward(gid(y + 3, zz), c, yp)
        else:
            arrive(gid(y + 1, zz), c)
            forward(gid(y + 1, zz), c, ym)

    def rest_y(zz, c):
        if c < half:
            arrive(gid(y + 1, zz), c)
        else:
            arrive(gid(y + 3, zz), c)
        arrive(gid(y + 2, zz), c)

    for c in order:
        second_y(z, c)
    behind = None
    for c in order:
        arrive(zm, c)
        if c < half:
            forward(zm, c, zp)
        forward(zm, c, yp)
        forward(zm, c, ym)
        arrive(zp, c)
        if c >= half:
            forward(zp, c, zm)
        forward(zp, c, yp)
        forward(zp, c, ym)
        if behind is not None:
            second_y(z + 1, behind)
            second_y(z + 3, behind)
        behind = c
    z2 = gid(y, z + 2)
    for c in order:
        arrive(z2, c)
        forward(z2, c, yp)
        forward(z2, c, ym)
        if behind is not None:
            second_y(z + 1, behind)
            second_y(z + 3, behind)
            behind = None
    for c in order:
        second_y(z + 2, c)
    own.wait()
    for zz in (z, z + 1, z + 3, z + 2):
        for c in order:
            rest_y(zz, c)
    for load in loads:
        load.wait()

    total = gath[g].astype(F32)
    count = cnt_ref[0]
    for t in range(TILES):
        live = jnp.where(t < count, 1.0, 0.0)
        chosen = gath[src_ref[0, t]]
        part = jnp.dot(
            tiles_v[:, t * ROWS:(t + 1) * ROWS], chosen, preferred_element_type=F32
        )
        total = total + part * live
    mean_square = jnp.mean(total * total, axis=-1, keepdims=True)
    normed = (total * lax.rsqrt(mean_square + 1e-6)).astype(BF16)
    for j in range(3):
        if j < 2:
            weight = wqk_v[:, j * D:(j + 1) * D]
        else:
            weight = wv_v[...]
        res = jnp.dot(normed, weight, preferred_element_type=F32)
        for u in range(D // 128):
            qkv_t[pl.ds(j * D + u * 128, 128), :] = res[:, u * 128:(u + 1) * 128].T
    bucket = jnp.broadcast_to(bucket_ref[...].astype(F32), (8, ROWS))
    for h in range(H):
        parts = [qkv_t[pl.ds(j * D + h * HD, HD), :] for j in range(3)]
        out_ref[h] = jnp.concatenate(parts + [bucket], axis=0).astype(BF16)
    for copy in sent:
        copy.wait_send()


def attention_kernel(
    piece_ref, bias_ref,
    out_ref,
    recv, kaug, qaug_t, vaug_t, s_a, s_b, o_send, o_recv,
    send_sem, recv_sem, osend_sem, orecv_sem, local_sem,
):
    me = lax.axis_index("seq")

    barrier = pltpu.get_barrier_semaphore()

    def greet(k, carry):
        peer = lax.rem(me + k, NS)
        pl.semaphore_signal(barrier, inc=1, device_id={"seq": peer}, device_id_type=MESH)
        return carry

    lax.fori_loop(1, NS, greet, 0)
    pl.semaphore_wait(barrier, NS - 1)

    def piece_copy(peer, slot):
        return pltpu.make_async_remote_copy(
            src_ref=piece_ref.at[peer],
            dst_ref=recv.at[slot],
            send_sem=send_sem.at[peer],
            recv_sem=recv_sem.at[slot],
            device_id={"seq": peer},
            device_id_type=MESH,
        )

    def send_piece(k, carry):
        piece_copy(lax.rem(me + k, NS), me).start()
        return carry

    lax.fori_loop(1, NS, send_piece, 0)
    own = pltpu.make_async_copy(piece_ref.at[me], recv.at[me], local_sem.at[0])
    own.start()

    row = bias_ref[pl.ds(me, 1), :] * LOG2E
    lane = lax.broadcasted_iota(jnp.int32, (NB, NB * NB), 1)
    sub = lax.broadcasted_iota(jnp.int32, (NB, NB * NB), 0)
    spread = jnp.where((lane & (NB - 1)) == sub, jnp.broadcast_to(row, (NB, NB * NB)), 0.0)
    top = spread.astype(BF16)
    left = spread - top.astype(F32)
    mid = left.astype(BF16)
    low = (left - mid.astype(F32)).astype(BF16)
    bias_rows = jnp.concatenate([top, mid, low], axis=0)
    row_bucket = (lax.broadcasted_iota(jnp.int32, (NB * NB, ROWS), 0) >> 4).astype(F32)
    row_index = lax.broadcasted_iota(jnp.int32, (NB, ROWS), 0).astype(F32)
    pad = jnp.zeros((32, ROWS), F32)
    ones = jnp.ones((8, ROWS), F32)

    def prepare(s):
        piece = recv[s].astype(F32)
        q, k, v = piece[0:24] * SCALE_LOG2, piece[24:48], piece[48:72]
        b = piece[72:73]
        q_top = q.astype(BF16).astype(F32)
        chosen = (jnp.broadcast_to(b, (NB * NB, ROWS)) == row_bucket).astype(F32).astype(BF16)
        q_bias = jnp.dot(bias_rows, chosen, preferred_element_type=F32)
        onehot = (jnp.broadcast_to(b, (NB, ROWS)) == row_index).astype(F32)
        off = pl.multiple_of(s * ROWS, ROWS)
        qaug_t[:, pl.ds(off, ROWS)] = jnp.concatenate(
            [q_top, q - q_top, q_bias, pad], axis=0
        ).astype(BF16)
        k_rows = jnp.concatenate([k, k, onehot, onehot, onehot, pad], axis=0)
        kaug[pl.ds(off, ROWS), :] = k_rows.T.astype(BF16)
        vaug_t[:, pl.ds(off, ROWS)] = jnp.concatenate([v, ones], axis=0).astype(BF16)

    own.wait()
    prepare(me)

    def take_piece(k, carry):
        slot = lax.rem(me + NS - k, NS)
        piece_copy(slot, slot).wait_recv()
        prepare(slot)
        return carry

    lax.fori_loop(1, NS, take_piece, 0)

    nq = NODES_G // QB

    def scores(i, j, dest, peak):
        off = pl.multiple_of(i * QB, QB)
        s = jnp.dot(
            kaug[pl.ds(j * KC, KC), :], qaug_t[:, pl.ds(off, QB)], preferred_element_type=F32
        )
        dest[pl.ds(j * KC, KC), :] = s
        return jnp.maximum(peak, jnp.max(s.reshape(KC // 8, 8, QB), axis=0))

    low_peak = jnp.full((8, QB), -3e38, F32)

    def step(i, peak_in, s_in, s_out):
        peak = jnp.max(peak_in, axis=0, keepdims=True)
        after = jnp.minimum(i + 1, nq - 1)
        peak_out = low_peak
        acc = jnp.zeros((32, QB), F32)
        for j in range(NODES_G // KC):
            peak_out = scores(after, j, s_out, peak_out)
            p = jnp.exp2(s_in[pl.ds(j * KC, KC), :] - peak).astype(BF16)
            acc = acc + jnp.dot(
                vaug_t[:, pl.ds(j * KC, KC)], p, preferred_element_type=F32
            )
        res = (acc / acc[24:25]).astype(BF16)
        for u in range(QB // ROWS):
            o_send[i * (QB // ROWS) + u] = res[:, u * ROWS:(u + 1) * ROWS]
        return peak_out

    def out_copy(owner, slot):
        return pltpu.make_async_remote_copy(
            src_ref=o_send.at[owner],
            dst_ref=o_recv.at[slot],
            send_sem=osend_sem.at[owner],
            recv_sem=orecv_sem.at[slot],
            device_id={"seq": owner},
            device_id_type=MESH,
        )

    def give(i):
        for u in range(QB // ROWS):
            owner = i * (QB // ROWS) + u

            @pl.when(owner != me)
            def _():
                out_copy(owner, me).start()

    peak = low_peak
    for j in range(NODES_G // KC):
        peak = scores(0, j, s_a, peak)

    def two(t, peak):
        peak = step(2 * t, peak, s_a, s_b)
        give(2 * t)
        peak = step(2 * t + 1, peak, s_b, s_a)
        give(2 * t + 1)
        return peak

    lax.fori_loop(0, nq // 2, two, peak)
    o_recv[me] = o_send[me]

    def take_out(k, carry):
        slot = lax.rem(me + NS - k, NS)
        out_copy(slot, slot).wait_recv()
        return carry

    lax.fori_loop(1, NS, take_out, 0)
    for h in range(H):
        out_ref[pl.ds(h * HD, HD), :] = o_recv[h].astype(F32)[0:HD]

    def drain(k, carry):
        peer = lax.rem(me + k, NS)
        piece_copy(peer, me).wait_send()
        out_copy(peer, me).wait_send()
        return carry

    lax.fori_loop(1, NS, drain, 0)


def on_device(features, tiles, tile_src, tile_count, node_bucket, w_qk, w_v, bias_table):
    hbm = pl.BlockSpec(memory_space=pl.ANY)
    vmem = pl.BlockSpec(memory_space=pltpu.VMEM)
    smem = pl.BlockSpec(memory_space=pltpu.SMEM)
    sends = 15 * CHUNKS
    pieces = pl.pallas_call(
        aggregate_kernel,
        out_shape=jax.ShapeDtypeStruct((H, PIECE, ROWS), BF16),
        in_specs=[hbm, hbm, smem, smem, vmem, hbm, hbm],
        out_specs=vmem,
        scratch_shapes=[
            pltpu.VMEM((NG, ROWS, D), BF16),
            pltpu.VMEM((ROWS, TILES * ROWS), BF16),
            pltpu.VMEM((D, 2 * D), BF16),
            pltpu.VMEM((D, D), BF16),
            pltpu.VMEM((3 * D, ROWS), F32),
            pltpu.SemaphoreType.DMA((sends,)),
            pltpu.SemaphoreType.DMA((NG, CHUNKS)),
            pltpu.SemaphoreType.DMA((4,)),
        ],
        compiler_params=pltpu.CompilerParams(
            collective_id=0, has_side_effects=True, vmem_limit_bytes=62 * 1024 * 1024
        ),
        name="aggregate",
    )(features, tiles, tile_src, tile_count, node_bucket.reshape(1, ROWS), w_qk, w_v)
    out_t = pl.pallas_call(
        attention_kernel,
        out_shape=jax.ShapeDtypeStruct((D, ROWS), F32),
        in_specs=[hbm, vmem],
        out_specs=vmem,
        scratch_shapes=[
            pltpu.VMEM((NS, PIECE, ROWS), BF16),
            pltpu.VMEM((NODES_G, 128), BF16),
            pltpu.VMEM((128, NODES_G), BF16),
            pltpu.VMEM((32, NODES_G), BF16),
            pltpu.VMEM((NODES_G, QB), F32),
            pltpu.VMEM((NODES_G, QB), F32),
            pltpu.VMEM((NS, 32, ROWS), BF16),
            pltpu.VMEM((NS, 32, ROWS), BF16),
            pltpu.SemaphoreType.DMA((NS,)),
            pltpu.SemaphoreType.DMA((NS,)),
            pltpu.SemaphoreType.DMA((NS,)),
            pltpu.SemaphoreType.DMA((NS,)),
            pltpu.SemaphoreType.DMA((1,)),
        ],
        compiler_params=pltpu.CompilerParams(
            collective_id=1, has_side_effects=True, vmem_limit_bytes=56 * 1024 * 1024
        ),
        name="attention",
    )(pieces, bias_table)
    return out_t.T.astype(BF16)


def solution(mesh):
    rows = P(("group", "seq"), None)
    line = P(("group", "seq"))
    return jax.shard_map(
        on_device,
        mesh=mesh,
        in_specs=(rows, rows, rows, line, line, P(), P(), P()),
        out_specs=rows,
        check_vma=False,
    )
```

```python
import functools
import math

import jax
import jax.numpy as jnp
from jax import lax
from jax.experimental import pallas as pl
from jax.experimental.pallas import tpu as pltpu
from jax.sharding import PartitionSpec as P

D = 768
H = 32
HD = 24
NB = 16
TILES = 8
ROWS = 128
NG = 16
NS = 32
NODES_G = ROWS * NS
KROWS = 32
CHUNKS = 4
CROWS = ROWS // CHUNKS
QB = 256
KC = 1024
SCALE_LOG2 = math.log2(math.e) / math.sqrt(HD)
LOG2E = math.log2(math.e)
MESH = pl.DeviceIdType.MESH
F32 = jnp.float32
BF16 = jnp.bfloat16


def layer_kernel(
    x_ref, tiles_ref, src_ref, cnt_ref, bucket_ref, wqk_ref, wv_ref, bias_ref,
    out_ref,
    gath, tiles_v, wqk_v, wv_v, qkv_t,
    k_send, v_send, q_send, k_recv, v_recv, q_recv, o_send, o_recv,
    kaug, vaug_t, q_even, q_odd, s_even, s_odd,
    gsend_sem, grecv_sem, local_sem,
    ksend_sem, krecv_sem, vsend_sem, vrecv_sem, qsend_sem, qrecv_sem, osend_sem, orecv_sem,
):
    g = lax.axis_index("group")
    me = lax.axis_index("seq")
    y = g // 4
    z = lax.rem(g, 4)

    def gid(yy, zz):
        return lax.rem(yy, 4) * 4 + lax.rem(zz, 4)

    zp, zm = gid(y, z + 1), gid(y, z + 3)
    yp, ym = gid(y + 1, z), gid(y + 3, z)

    barrier = pltpu.get_barrier_semaphore()
    for peer in (zp, zm, yp, ym):
        pl.semaphore_signal(barrier, inc=1, device_id={"group": peer}, device_id_type=MESH)

    def greet(k, carry):
        peer = lax.rem(me + k, NS)
        pl.semaphore_signal(barrier, inc=1, device_id={"seq": peer}, device_id_type=MESH)
        return carry

    lax.fori_loop(1, NS, greet, 0)

    own = pltpu.make_async_copy(x_ref, gath.at[g], local_sem.at[0])
    own.start()
    loads = [
        pltpu.make_async_copy(tiles_ref, tiles_v, local_sem.at[1]),
        pltpu.make_async_copy(wqk_ref, wqk_v, local_sem.at[2]),
        pltpu.make_async_copy(wv_ref, wv_v, local_sem.at[3]),
    ]
    for load in loads:
        load.start()
    pl.semaphore_wait(barrier, 4 + NS - 1)

    sent = []

    def block(origin, c):
        return gath.at[origin, pl.ds(c * CROWS, CROWS), :]

    def send(source, origin, c, peer):
        copy = pltpu.make_async_remote_copy(
            src_ref=source,
            dst_ref=block(origin, c),
            send_sem=gsend_sem.at[len(sent)],
            recv_sem=grecv_sem.at[origin, c],
            device_id={"group": peer},
            device_id_type=MESH,
        )
        copy.start()
        sent.append(copy)

    def first(c, peer):
        send(x_ref.at[pl.ds(c * CROWS, CROWS), :], g, c, peer)

    def forward(origin, c, peer):
        send(block(origin, c), origin, c, peer)

    arrived = set()

    def arrive(dy, dz, c):
        arrived.add((dy, dz, c))
        origin = gid(y + dy, z + dz)
        pltpu.make_async_remote_copy(
            src_ref=block(origin, c),
            dst_ref=block(origin, c),
            send_sem=gsend_sem.at[0],
            recv_sem=grecv_sem.at[origin, c],
            device_id={"group": zp},
            device_id_type=MESH,
        ).wait_recv()

    half = CHUNKS // 2
    upper = list(range(half))
    lower = list(range(CHUNKS - 1, half - 1, -1))
    pending = []

    def across(dz, c):
        forward(gid(y, z + dz), c, yp)
        forward(gid(y, z + dz), c, ym)
        pending.append((dz, c))

    def catch_up(keep):
        while len(pending) > keep:
            dz, c = pending.pop(0)
            dy, peer = (3, yp) if c < half else (1, ym)
            arrive(dy, dz, c)
            forward(gid(y + dy, z + dz), c, peer)

    for t, b in zip(upper, lower):
        first(b, zp)
        first(t, zm)
    for t, b in zip(upper, lower):
        first(t, zp)
        first(b, zm)
    for t, b in zip(upper, lower):
        for c in (t, b):
            first(c, yp)
            first(c, ym)
            pending.append((0, c))
    for t, b in zip(upper, lower):
        arrive(0, 3, b)
        across(3, b)
        arrive(0, 1, t)
        across(1, t)
        catch_up(2)
    for t, b in zip(upper, lower):
        arrive(0, 3, t)
        forward(zm, t, zp)
        arrive(0, 1, b)
        forward(zp, b, zm)
        across(3, t)
        across(1, b)
        catch_up(2)
    for t, b in zip(upper, lower):
        arrive(0, 2, t)
        across(2, t)
        arrive(0, 2, b)
        across(2, b)
        catch_up(2)
    catch_up(0)
    own.wait()
    for load in loads:
        load.wait()
    for dz in (0, 1, 3, 2):
        for dy in (1, 3, 2):
            for c in range(CHUNKS):
                if (dy, dz, c) not in arrived:
                    arrive(dy, dz, c)

    total = gath[g].astype(F32)
    count = cnt_ref[0]
    for t in range(TILES):
        live = jnp.where(t < count, 1.0, 0.0)
        chosen = gath[src_ref[0, t]]
        part = jnp.dot(
            tiles_v[:, t * ROWS:(t + 1) * ROWS], chosen, preferred_element_type=F32
        )
        total = total + part * live
    mean_square = jnp.mean(total * total, axis=-1, keepdims=True)
    normed = (total * lax.rsqrt(mean_square + 1e-6)).astype(BF16)
    bucket = jnp.broadcast_to(bucket_ref[...].astype(F32), (8, ROWS))

    def exchange(source, dest, send_sem, recv_sem):
        def copy(peer, slot):
            return pltpu.make_async_remote_copy(
                src_ref=source.at[peer],
                dst_ref=dest.at[slot],
                send_sem=send_sem.at[peer],
                recv_sem=recv_sem.at[slot],
                device_id={"seq": peer},
                device_id_type=MESH,
            )

        return copy

    k_copy = exchange(k_send, k_recv, ksend_sem, krecv_sem)
    v_copy = exchange(v_send, v_recv, vsend_sem, vrecv_sem)
    q_copy = exchange(q_send, q_recv, qsend_sem, qrecv_sem)
    o_copy = exchange(o_send, o_recv, osend_sem, orecv_sem)

    def project(weight, dest, recv, copy, extra):
        res = jnp.dot(normed, weight, preferred_element_type=F32)
        for u in range(D // 128):
            qkv_t[pl.ds(u * 128, 128), :] = res[:, u * 128:(u + 1) * 128].T
        for h in range(H):
            rows = qkv_t[pl.ds(h * HD, HD), :]
            if extra is not None:
                rows = jnp.concatenate([rows, extra], axis=0)
            dest[h] = rows.astype(BF16)

        def scatter(k, carry):
            copy(lax.rem(me + k, NS), me).start()
            return carry

        lax.fori_loop(1, NS, scatter, 0)
        recv[me] = dest[me]

    project(wqk_v[:, D:2 * D], k_send, k_recv, k_copy, bucket)
    project(wv_v[...], v_send, v_recv, v_copy, None)
    project(wqk_v[:, 0:D], q_send, q_recv, q_copy, None)

    row = bias_ref[pl.ds(me, 1), :] * LOG2E
    lane = lax.broadcasted_iota(jnp.int32, (NB, NB * NB), 1)
    sub = lax.broadcasted_iota(jnp.int32, (NB, NB * NB), 0)
    spread = jnp.where((lane & (NB - 1)) == sub, jnp.broadcast_to(row, (NB, NB * NB)), 0.0)
    top = spread.astype(BF16)
    left = spread - top.astype(F32)
    mid = left.astype(BF16)
    low = (left - mid.astype(F32)).astype(BF16)
    bias_rows = jnp.concatenate([top, mid, low], axis=0)
    row_bucket = (lax.broadcasted_iota(jnp.int32, (NB * NB, ROWS), 0) >> 4).astype(F32)
    row_index = lax.broadcasted_iota(jnp.int32, (NB, ROWS), 0).astype(F32)
    pad = jnp.zeros((32, ROWS), F32)
    ones = jnp.ones((8, ROWS), F32)

    def prepare_kv(s):
        k_piece = k_recv[s].astype(F32)
        k, b = k_piece[0:HD], k_piece[HD:HD + 1]
        onehot = (jnp.broadcast_to(b, (NB, ROWS)) == row_index).astype(F32)
        off = pl.multiple_of(s * ROWS, ROWS)
        k_rows = jnp.concatenate([k, k, onehot, onehot, onehot, pad], axis=0)
        kaug[pl.ds(off, ROWS), :] = k_rows.T.astype(BF16)
        v = v_recv[s].astype(F32)
        vaug_t[:, pl.ds(off, ROWS)] = jnp.concatenate([v, ones], axis=0).astype(BF16)

    def take_kv(k, carry):
        slot = lax.rem(me + NS - k, NS)
        k_copy(slot, slot).wait_recv()
        v_copy(slot, slot).wait_recv()
        prepare_kv(slot)
        return carry

    prepare_kv(me)
    lax.fori_loop(1, NS, take_kv, 0)

    nq = NODES_G // QB
    per = QB // ROWS
    start = me // per

    def owner_of(i, u):
        return lax.rem(start + i, nq) * per + u

    def wait_q(i):
        for u in range(per):
            slot = owner_of(i, u)

            @pl.when((slot != me) & (i < nq))
            def _():
                q_copy(slot, slot).wait_recv()

    def prepare_q(i, dest):
        for u in range(per):
            slot = owner_of(i, u)
            q = q_recv[slot].astype(F32) * SCALE_LOG2
            b = k_recv[slot].astype(F32)[HD:HD + 1]
            q_top = q.astype(BF16).astype(F32)
            chosen = (jnp.broadcast_to(b, (NB * NB, ROWS)) == row_bucket).astype(F32)
            q_bias = jnp.dot(bias_rows, chosen.astype(BF16), preferred_element_type=F32)
            dest[:, u * ROWS:(u + 1) * ROWS] = jnp.concatenate(
                [q_top, q - q_top, q_bias, pad], axis=0
            ).astype(BF16)

    def scores(j, q_now, dest, peak):
        s = jnp.dot(kaug[pl.ds(j * KC, KC), :], q_now[...], preferred_element_type=F32)
        dest[pl.ds(j * KC, KC), :] = s
        return jnp.maximum(peak, jnp.max(s.reshape(KC // 8, 8, QB), axis=0))

    low_peak = jnp.full((8, QB), -3e38, F32)

    def step(i, peak_in, s_in, s_out, q_after, q_later):
        wait_q(i + 2)
        peak = jnp.max(peak_in, axis=0, keepdims=True)
        peak_out = low_peak
        acc = jnp.zeros((32, QB), F32)
        for j in range(NODES_G // KC):
            peak_out = scores(j, q_after, s_out, peak_out)
            p = jnp.exp2(s_in[pl.ds(j * KC, KC), :] - peak).astype(BF16)
            acc = acc + jnp.dot(
                vaug_t[:, pl.ds(j * KC, KC)], p, preferred_element_type=F32
            )
        prepare_q(i + 2, q_later)
        res = (acc[0:HD] / acc[HD:HD + 1]).astype(BF16)
        for u in range(per):
            o_send[owner_of(i, u)] = res[:, u * ROWS:(u + 1) * ROWS]
        for u in range(per):
            owner = owner_of(i, u)

            @pl.when(owner != me)
            def _():
                o_copy(owner, me).start()

        return peak_out

    wait_q(0)
    wait_q(1)
    prepare_q(0, q_even)
    prepare_q(1, q_odd)
    peak = low_peak
    for j in range(NODES_G // KC):
        peak = scores(j, q_even, s_even, peak)

    def two(t, peak):
        peak = step(2 * t, peak, s_even, s_odd, q_odd, q_even)
        return step(2 * t + 1, peak, s_odd, s_even, q_even, q_odd)

    lax.fori_loop(0, nq // 2, two, peak)
    o_recv[me] = o_send[me]

    def take_out(k, carry):
        slot = lax.rem(me + NS - k, NS)
        o_copy(slot, slot).wait_recv()
        return carry

    lax.fori_loop(1, NS, take_out, 0)
    for h in range(H):
        qkv_t[pl.ds(h * HD, HD), :] = o_recv[h].astype(F32)
    for u in range(D // 128):
        out_ref[:, u * 128:(u + 1) * 128] = qkv_t[pl.ds(u * 128, 128), :].T.astype(BF16)

    def drain(k, carry):
        peer = lax.rem(me + k, NS)
        for copy in (k_copy, v_copy, q_copy, o_copy):
            copy(peer, me).wait_send()
        return carry

    lax.fori_loop(1, NS, drain, 0)
    for copy in sent:
        copy.wait_send()


def on_device(features, tiles, tile_src, tile_count, node_bucket, w_qk, w_v, bias_table):
    hbm = pl.BlockSpec(memory_space=pl.ANY)
    vmem = pl.BlockSpec(memory_space=pltpu.VMEM)
    smem = pl.BlockSpec(memory_space=pltpu.SMEM)
    dma = pltpu.SemaphoreType.DMA
    return pl.pallas_call(
        layer_kernel,
        out_shape=jax.ShapeDtypeStruct((ROWS, D), BF16),
        in_specs=[hbm, hbm, smem, smem, vmem, hbm, hbm, vmem],
        out_specs=vmem,
        scratch_shapes=[
            pltpu.VMEM((NG, ROWS, D), BF16),
            pltpu.VMEM((ROWS, TILES * ROWS), BF16),
            pltpu.VMEM((D, 2 * D), BF16),
            pltpu.VMEM((D, D), BF16),
            pltpu.VMEM((D, ROWS), F32),
            pltpu.VMEM((NS, KROWS, ROWS), BF16),
            pltpu.VMEM((NS, HD, ROWS), BF16),
            pltpu.VMEM((NS, HD, ROWS), BF16),
            pltpu.VMEM((NS, KROWS, ROWS), BF16),
            pltpu.VMEM((NS, HD, ROWS), BF16),
            pltpu.VMEM((NS, HD, ROWS), BF16),
            pltpu.VMEM((NS, HD, ROWS), BF16),
            pltpu.VMEM((NS, HD, ROWS), BF16),
            pltpu.VMEM((NODES_G, 128), BF16),
            pltpu.VMEM((32, NODES_G), BF16),
            pltpu.VMEM((128, QB), BF16),
            pltpu.VMEM((128, QB), BF16),
            pltpu.VMEM((NODES_G, QB), F32),
            pltpu.VMEM((NODES_G, QB), F32),
            dma((15 * CHUNKS,)),
            dma((NG, CHUNKS)),
            dma((4,)),
        ] + [dma((NS,)) for _ in range(8)],
        compiler_params=pltpu.CompilerParams(
            collective_id=0, has_side_effects=True, vmem_limit_bytes=62 * 1024 * 1024
        ),
        name="layer",
    )(features, tiles, tile_src, tile_count, node_bucket.reshape(1, ROWS), w_qk, w_v, bias_table)


def solution(mesh):
    rows = P(("group", "seq"), None)
    line = P(("group", "seq"))
    return jax.shard_map(
        on_device,
        mesh=mesh,
        in_specs=(rows, rows, rows, line, line, P(), P(), P()),
        out_specs=rows,
        check_vma=False,
    )
```

```python
import functools
import math

import jax
import jax.numpy as jnp
from jax import lax
from jax.experimental import pallas as pl
from jax.experimental.pallas import tpu as pltpu
from jax.sharding import PartitionSpec as P

D = 768
H = 32
HD = 24
NB = 16
TILES = 8
ROWS = 128
NG = 16
NS = 32
NODES_G = ROWS * NS
HELD = 8
CHUNKS = 4
CROWS = ROWS // CHUNKS
QB = 256
KC = 1024
SCALE_LOG2 = math.log2(math.e) / math.sqrt(HD)
LOG2E = math.log2(math.e)
MESH = pl.DeviceIdType.MESH
F32 = jnp.float32
BF16 = jnp.bfloat16


def layer_kernel(
    x_ref, tiles_ref, src_ref, cnt_ref, bucket_ref, wqk_ref, wv_ref, bias_ref,
    out_ref,
    gath, tiles_v, wqk_v, wv_v, qkv_t,
    b_recv, k_send, v_send, q_send, k_recv, v_recv, q_recv, o_send, o_recv,
    kaug, vaug_t, q_all, s_all, peaks,
    gsend_sem, grecv_sem, local_sem, bsend_sem, brecv_sem,
    ksend_sem, krecv_sem, vsend_sem, vrecv_sem, qsend_sem, qrecv_sem, osend_sem, orecv_sem,
):
    g = lax.axis_index("group")
    me = lax.axis_index("seq")
    y = g // 4
    z = lax.rem(g, 4)

    def gid(yy, zz):
        return lax.rem(yy, 4) * 4 + lax.rem(zz, 4)

    zp, zm = gid(y, z + 1), gid(y, z + 3)
    yp, ym = gid(y + 1, z), gid(y + 3, z)

    barrier = pltpu.get_barrier_semaphore()
    for peer in (zp, zm, yp, ym):
        pl.semaphore_signal(barrier, inc=1, device_id={"group": peer}, device_id_type=MESH)

    def greet(k, carry):
        peer = lax.rem(me + k, NS)
        pl.semaphore_signal(barrier, inc=1, device_id={"seq": peer}, device_id_type=MESH)
        return carry

    lax.fori_loop(1, NS, greet, 0)

    own = pltpu.make_async_copy(x_ref, gath.at[g], local_sem.at[0])
    own.start()
    loads = [
        pltpu.make_async_copy(tiles_ref, tiles_v, local_sem.at[1]),
        pltpu.make_async_copy(wqk_ref, wqk_v, local_sem.at[2]),
        pltpu.make_async_copy(wv_ref, wv_v, local_sem.at[3]),
    ]
    for load in loads:
        load.start()
    pl.semaphore_wait(barrier, 4 + NS - 1)

    sent = []

    def block(origin, c):
        return gath.at[origin, pl.ds(c * CROWS, CROWS), :]

    def send(source, origin, c, peer):
        copy = pltpu.make_async_remote_copy(
            src_ref=source,
            dst_ref=block(origin, c),
            send_sem=gsend_sem.at[len(sent)],
            recv_sem=grecv_sem.at[origin, c],
            device_id={"group": peer},
            device_id_type=MESH,
        )
        copy.start()
        sent.append(copy)

    def first(c, peer):
        send(x_ref.at[pl.ds(c * CROWS, CROWS), :], g, c, peer)

    def forward(origin, c, peer):
        send(block(origin, c), origin, c, peer)

    arrived = set()

    def arrive(dy, dz, c):
        arrived.add((dy, dz, c))
        origin = gid(y + dy, z + dz)
        pltpu.make_async_remote_copy(
            src_ref=block(origin, c),
            dst_ref=block(origin, c),
            send_sem=gsend_sem.at[0],
            recv_sem=grecv_sem.at[origin, c],
            device_id={"group": zp},
            device_id_type=MESH,
        ).wait_recv()

    half = CHUNKS // 2
    upper = list(range(half))
    lower = list(range(CHUNKS - 1, half - 1, -1))
    pending = []

    def across(dz, c):
        forward(gid(y, z + dz), c, yp)
        forward(gid(y, z + dz), c, ym)
        pending.append((dz, c))

    def catch_up(keep):
        while len(pending) > keep:
            dz, c = pending.pop(0)
            dy, peer = (3, yp) if c < half else (1, ym)
            arrive(dy, dz, c)
            forward(gid(y + dy, z + dz), c, peer)

    for t, b in zip(upper, lower):
        first(b, zp)
        first(t, zm)
    for t, b in zip(upper, lower):
        first(t, zp)
        first(b, zm)
    for t, b in zip(upper, lower):
        for c in (t, b):
            first(c, yp)
            first(c, ym)
            pending.append((0, c))

    def b_copy(peer, slot):
        return pltpu.make_async_remote_copy(
            src_ref=bucket_ref,
            dst_ref=b_recv.at[slot],
            send_sem=bsend_sem.at[peer],
            recv_sem=brecv_sem.at[slot],
            device_id={"seq": peer},
            device_id_type=MESH,
        )

    def send_bucket(k, carry):
        b_copy(lax.rem(me + k, NS), me).start()
        return carry

    lax.fori_loop(1, NS, send_bucket, 0)
    b_recv[me] = bucket_ref[...]
    for t, b in zip(upper, lower):
        arrive(0, 3, b)
        across(3, b)
        arrive(0, 1, t)
        across(1, t)
        catch_up(2)
    for t, b in zip(upper, lower):
        arrive(0, 3, t)
        forward(zm, t, zp)
        arrive(0, 1, b)
        forward(zp, b, zm)
        across(3, t)
        across(1, b)
        catch_up(2)
    for t, b in zip(upper, lower):
        arrive(0, 2, t)
        across(2, t)
        arrive(0, 2, b)
        across(2, b)
        catch_up(2)
    catch_up(0)
    own.wait()
    for load in loads:
        load.wait()
    for dz in (0, 1, 3, 2):
        for dy in (1, 3, 2):
            for c in range(CHUNKS):
                if (dy, dz, c) not in arrived:
                    arrive(dy, dz, c)

    total = gath[g].astype(F32)
    count = cnt_ref[0]
    for t in range(TILES):
        live = jnp.where(t < count, 1.0, 0.0)
        chosen = gath[src_ref[0, t]]
        part = jnp.dot(
            tiles_v[:, t * ROWS:(t + 1) * ROWS], chosen, preferred_element_type=F32
        )
        total = total + part * live
    mean_square = jnp.mean(total * total, axis=-1, keepdims=True)
    normed = (total * lax.rsqrt(mean_square + 1e-6)).astype(BF16)

    def exchange(source, dest, send_sem, recv_sem):
        def copy(peer, slot):
            return pltpu.make_async_remote_copy(
                src_ref=source.at[peer],
                dst_ref=dest.at[slot],
                send_sem=send_sem.at[peer],
                recv_sem=recv_sem.at[slot],
                device_id={"seq": peer},
                device_id_type=MESH,
            )

        return copy

    k_copy = exchange(k_send, k_recv, ksend_sem, krecv_sem)
    v_copy = exchange(v_send, v_recv, vsend_sem, vrecv_sem)
    q_copy = exchange(q_send, q_recv, qsend_sem, qrecv_sem)
    o_copy = exchange(o_send, o_recv, osend_sem, orecv_sem)

    def project(weight, dest, recv, copy, sign):
        res = jnp.dot(normed, weight, preferred_element_type=F32)
        for u in range(D // 128):
            qkv_t[pl.ds(u * 128, 128), :] = res[:, u * 128:(u + 1) * 128].T
        for h in range(H):
            dest[h] = qkv_t[pl.ds(h * HD, HD), :].astype(BF16)

        def scatter(k, carry):
            copy(lax.rem(me + NS + sign * k, NS), me).start()
            return carry

        lax.fori_loop(1, NS, scatter, 0)
        recv[me] = dest[me]

    project(wqk_v[:, D:2 * D], k_send, k_recv, k_copy, 1)
    project(wqk_v[:, 0:D], q_send, q_recv, q_copy, -1)
    project(wv_v[...], v_send, v_recv, v_copy, 1)

    row = bias_ref[pl.ds(me, 1), :] * LOG2E
    lane = lax.broadcasted_iota(jnp.int32, (NB, NB * NB), 1)
    sub = lax.broadcasted_iota(jnp.int32, (NB, NB * NB), 0)
    spread = jnp.where((lane & (NB - 1)) == sub, jnp.broadcast_to(row, (NB, NB * NB)), 0.0)
    top = spread.astype(BF16)
    left = spread - top.astype(F32)
    mid = left.astype(BF16)
    low = (left - mid.astype(F32)).astype(BF16)
    bias_rows = jnp.concatenate([top, mid, low], axis=0)
    row_bucket = (lax.broadcasted_iota(jnp.int32, (NB * NB, ROWS), 0) >> 4).astype(F32)
    row_index = lax.broadcasted_iota(jnp.int32, (NB, ROWS), 0).astype(F32)
    pad = jnp.zeros((32, ROWS), F32)

    def prepare_k(s):
        k = k_recv[s].astype(F32)
        onehot = (jnp.broadcast_to(b_recv[s].astype(F32), (NB, ROWS)) == row_index).astype(F32)
        off = pl.multiple_of(s * ROWS, ROWS)
        k_rows = jnp.concatenate([k, k, onehot, onehot, onehot, pad], axis=0)
        kaug[pl.ds(off, ROWS), :] = k_rows.T.astype(BF16)

    def take_k(k, carry):
        slot = lax.rem(me + NS - k, NS)
        b_copy(slot, slot).wait_recv()
        k_copy(slot, slot).wait_recv()
        prepare_k(slot)
        return carry

    prepare_k(me)
    lax.fori_loop(1, NS, take_k, 0)

    nq = NODES_G // QB
    per = QB // ROWS
    start = me // per

    def owner_of(i, u):
        return lax.rem(start + i, nq) * per + u

    def wait_q(i):
        for u in range(per):
            slot = owner_of(i, u)

            @pl.when((slot != me) & (i < nq))
            def _():
                q_copy(slot, slot).wait_recv()

    def prepare_q(i):
        for u in range(per):
            slot = owner_of(i, u)
            q = q_recv[slot].astype(F32) * SCALE_LOG2
            b = b_recv[slot].astype(F32)
            q_top = q.astype(BF16).astype(F32)
            chosen = (jnp.broadcast_to(b, (NB * NB, ROWS)) == row_bucket).astype(F32)
            q_bias = jnp.dot(bias_rows, chosen.astype(BF16), preferred_element_type=F32)
            q_all[i, :, u * ROWS:(u + 1) * ROWS] = jnp.concatenate(
                [q_top, q - q_top, q_bias, pad], axis=0
            ).astype(BF16)

    low_peak = jnp.full((8, QB), -3e38, F32)

    def scores(i, j, slot, peak):
        s = jnp.dot(kaug[pl.ds(j * KC, KC), :], q_all[i], preferred_element_type=F32)
        s_all[slot, pl.ds(j * KC, KC), :] = s
        return jnp.maximum(peak, jnp.max(s.reshape(KC // 8, 8, QB), axis=0))

    def early(i, carry):
        wait_q(i + 1)
        peak = low_peak
        for j in range(NODES_G // KC):
            peak = scores(i, j, i, peak)
        prepare_q(i + 1)
        peaks[i] = peak
        return carry

    def step(i, slot, after):
        if after:
            wait_q(i + HELD + 1)
        peak = jnp.max(peaks[i], axis=0, keepdims=True) - 2.0
        peak_out = low_peak
        acc = jnp.zeros((32, QB), F32)
        for j in range(NODES_G // KC):
            p = jnp.exp2((s_all[slot, pl.ds(j * KC, KC), :] - peak).astype(BF16))
            acc = acc + jnp.dot(
                vaug_t[:, pl.ds(j * KC, KC)], p, preferred_element_type=F32
            )
            if after:
                peak_out = scores(i + HELD, j, slot, peak_out)
        if after:
            prepare_q(i + HELD + 1)
            peaks[i + HELD] = peak_out
        res = (acc[0:HD] / acc[HD:HD + 1]).astype(BF16)
        for u in range(per):
            o_send[owner_of(i, u)] = res[:, u * ROWS:(u + 1) * ROWS]
        for u in range(per):
            owner = owner_of(i, u)

            @pl.when(owner != me)
            def _():
                o_copy(owner, me).start()

    def with_scores(i, carry):
        step(i, i, True)
        return carry

    def without_scores(i, carry):
        step(i, i - HELD, False)
        return carry

    def place_v(s):
        off = pl.multiple_of(s * ROWS, ROWS)
        vaug_t[0:HD, pl.ds(off, ROWS)] = v_recv[s]

    def take_v(k, carry):
        slot = lax.rem(me + NS - k, NS)
        v_copy(slot, slot).wait_recv()
        place_v(slot)
        return carry

    wait_q(0)
    prepare_q(0)
    lax.fori_loop(0, HELD, early, 0)
    vaug_t[...] = jnp.ones((32, NODES_G), BF16)
    place_v(me)
    lax.fori_loop(1, NS, take_v, 0)
    lax.fori_loop(0, nq - HELD, with_scores, 0)
    lax.fori_loop(nq - HELD, nq, without_scores, 0)
    o_recv[me] = o_send[me]

    def take_out(k, carry):
        slot = lax.rem(me + NS - k, NS)
        o_copy(slot, slot).wait_recv()
        return carry

    lax.fori_loop(1, NS, take_out, 0)
    for h in range(H):
        qkv_t[pl.ds(h * HD, HD), :] = o_recv[h].astype(F32)
    for u in range(D // 128):
        out_ref[:, u * 128:(u + 1) * 128] = qkv_t[pl.ds(u * 128, 128), :].T.astype(BF16)

    def drain(k, carry):
        peer = lax.rem(me + k, NS)
        for copy in (b_copy, k_copy, v_copy, q_copy, o_copy):
            copy(peer, me).wait_send()
        return carry

    lax.fori_loop(1, NS, drain, 0)
    for copy in sent:
        copy.wait_send()


def on_device(features, tiles, tile_src, tile_count, node_bucket, w_qk, w_v, bias_table):
    hbm = pl.BlockSpec(memory_space=pl.ANY)
    vmem = pl.BlockSpec(memory_space=pltpu.VMEM)
    smem = pl.BlockSpec(memory_space=pltpu.SMEM)
    dma = pltpu.SemaphoreType.DMA
    return pl.pallas_call(
        layer_kernel,
        out_shape=jax.ShapeDtypeStruct((ROWS, D), BF16),
        in_specs=[hbm, hbm, smem, smem, vmem, hbm, hbm, vmem],
        out_specs=vmem,
        scratch_shapes=[
            pltpu.VMEM((NG, ROWS, D), BF16),
            pltpu.VMEM((ROWS, TILES * ROWS), BF16),
            pltpu.VMEM((D, 2 * D), BF16),
            pltpu.VMEM((D, D), BF16),
            pltpu.VMEM((D, ROWS), F32),
            pltpu.VMEM((NS, 1, ROWS), jnp.int32),
        ] + [pltpu.VMEM((NS, HD, ROWS), BF16) for _ in range(8)] + [
            pltpu.VMEM((NODES_G, 128), BF16),
            pltpu.VMEM((32, NODES_G), BF16),
            pltpu.VMEM((NODES_G // QB + 1, 128, QB), BF16),
            pltpu.VMEM((HELD, NODES_G, QB), F32),
            pltpu.VMEM((NODES_G // QB, 8, QB), F32),
            dma((15 * CHUNKS,)),
            dma((NG, CHUNKS)),
            dma((4,)),
        ] + [dma((NS,)) for _ in range(10)],
        compiler_params=pltpu.CompilerParams(
            collective_id=0, has_side_effects=True, vmem_limit_bytes=62 * 1024 * 1024
        ),
        name="layer",
    )(features, tiles, tile_src, tile_count, node_bucket.reshape(1, ROWS), w_qk, w_v, bias_table)


def solution(mesh):
    rows = P(("group", "seq"), None)
    line = P(("group", "seq"))
    return jax.shard_map(
        on_device,
        mesh=mesh,
        in_specs=(rows, rows, rows, line, line, P(), P(), P()),
        out_specs=rows,
        check_vma=False,
    )
```

```python
import functools
import math

import jax
import jax.numpy as jnp
from jax import lax
from jax.experimental import pallas as pl
from jax.experimental.pallas import tpu as pltpu
from jax.sharding import PartitionSpec as P

D = 768
H = 32
HD = 24
NB = 16
TILES = 8
ROWS = 128
NG = 16
NS = 32
NODES_G = ROWS * NS
HELD = 8
CHUNKS = 4
CROWS = ROWS // CHUNKS
QB = 256
KC = 1024
SCALE_LOG2 = math.log2(math.e) / math.sqrt(HD)
LOG2E = math.log2(math.e)
MESH = pl.DeviceIdType.MESH
F32 = jnp.float32
BF16 = jnp.bfloat16


def layer_kernel(
    x_ref, tiles_ref, src_ref, cnt_ref, bucket_ref, wqk_ref, wv_ref, bias_ref,
    out_ref,
    gath, tiles_v, wqk_v, wv_v, qkv_t,
    b_recv, k_send, k_recv, qv_send, qv_recv, o_send, o_recv,
    kaug, vaug_t, q_all, s_all, peaks,
    gsend_sem, grecv_sem, local_sem, bsend_sem, brecv_sem,
    ksend_sem, krecv_sem, qvsend_sem, qvrecv_sem, osend_sem, orecv_sem,
):
    g = lax.axis_index("group")
    me = lax.axis_index("seq")
    y = g // 4
    z = lax.rem(g, 4)

    def gid(yy, zz):
        return lax.rem(yy, 4) * 4 + lax.rem(zz, 4)

    zp, zm = gid(y, z + 1), gid(y, z + 3)
    yp, ym = gid(y + 1, z), gid(y + 3, z)

    barrier = pltpu.get_barrier_semaphore()
    for peer in (zp, zm, yp, ym):
        pl.semaphore_signal(barrier, inc=1, device_id={"group": peer}, device_id_type=MESH)

    def greet(k, carry):
        peer = lax.rem(me + k, NS)
        pl.semaphore_signal(barrier, inc=1, device_id={"seq": peer}, device_id_type=MESH)
        return carry

    lax.fori_loop(1, NS, greet, 0)

    own = pltpu.make_async_copy(x_ref, gath.at[g], local_sem.at[0])
    own.start()
    loads = [
        pltpu.make_async_copy(tiles_ref, tiles_v, local_sem.at[1]),
        pltpu.make_async_copy(wqk_ref, wqk_v, local_sem.at[2]),
        pltpu.make_async_copy(wv_ref, wv_v, local_sem.at[3]),
    ]
    for load in loads:
        load.start()
    pl.semaphore_wait(barrier, 4 + NS - 1)

    sent = []

    def block(origin, c):
        return gath.at[origin, pl.ds(c * CROWS, CROWS), :]

    def send(source, origin, c, peer):
        copy = pltpu.make_async_remote_copy(
            src_ref=source,
            dst_ref=block(origin, c),
            send_sem=gsend_sem.at[len(sent)],
            recv_sem=grecv_sem.at[origin, c],
            device_id={"group": peer},
            device_id_type=MESH,
        )
        copy.start()
        sent.append(copy)

    def first(c, peer):
        send(x_ref.at[pl.ds(c * CROWS, CROWS), :], g, c, peer)

    def forward(origin, c, peer):
        send(block(origin, c), origin, c, peer)

    arrived = set()

    def arrive(dy, dz, c):
        arrived.add((dy, dz, c))
        origin = gid(y + dy, z + dz)
        pltpu.make_async_remote_copy(
            src_ref=block(origin, c),
            dst_ref=block(origin, c),
            send_sem=gsend_sem.at[0],
            recv_sem=grecv_sem.at[origin, c],
            device_id={"group": zp},
            device_id_type=MESH,
        ).wait_recv()

    half = CHUNKS // 2
    upper = list(range(half))
    lower = list(range(CHUNKS - 1, half - 1, -1))
    pending = []

    def across(dz, c):
        forward(gid(y, z + dz), c, yp)
        forward(gid(y, z + dz), c, ym)
        pending.append((dz, c))

    def catch_up(keep):
        while len(pending) > keep:
            dz, c = pending.pop(0)
            dy, peer = (3, yp) if c < half else (1, ym)
            arrive(dy, dz, c)
            forward(gid(y + dy, z + dz), c, peer)

    for t, b in zip(upper, lower):
        first(b, zp)
        first(t, zm)
    for t, b in zip(upper, lower):
        first(t, zp)
        first(b, zm)
    for t, b in zip(upper, lower):
        for c in (t, b):
            first(c, yp)
            first(c, ym)
            pending.append((0, c))

    def b_copy(peer, slot):
        return pltpu.make_async_remote_copy(
            src_ref=bucket_ref,
            dst_ref=b_recv.at[slot],
            send_sem=bsend_sem.at[peer],
            recv_sem=brecv_sem.at[slot],
            device_id={"seq": peer},
            device_id_type=MESH,
        )

    def send_bucket(k, carry):
        b_copy(lax.rem(me + k, NS), me).start()
        return carry

    lax.fori_loop(1, NS, send_bucket, 0)
    b_recv[me] = bucket_ref[...]
    for t, b in zip(upper, lower):
        arrive(0, 3, b)
        across(3, b)
        arrive(0, 1, t)
        across(1, t)
        catch_up(2)
    for t, b in zip(upper, lower):
        arrive(0, 3, t)
        forward(zm, t, zp)
        arrive(0, 1, b)
        forward(zp, b, zm)
        across(3, t)
        across(1, b)
        catch_up(2)
    for t, b in zip(upper, lower):
        arrive(0, 2, t)
        across(2, t)
        arrive(0, 2, b)
        across(2, b)
        catch_up(2)
    catch_up(0)
    own.wait()
    for load in loads:
        load.wait()
    for dz in (0, 1, 3, 2):
        for dy in (1, 3, 2):
            for c in range(CHUNKS):
                if (dy, dz, c) not in arrived:
                    arrive(dy, dz, c)

    total = gath[g].astype(F32)
    count = cnt_ref[0]
    for t in range(TILES):
        live = jnp.where(t < count, 1.0, 0.0)
        chosen = gath[src_ref[0, t]]
        part = jnp.dot(
            tiles_v[:, t * ROWS:(t + 1) * ROWS], chosen, preferred_element_type=F32
        )
        total = total + part * live
    mean_square = jnp.mean(total * total, axis=-1, keepdims=True)
    normed = (total * lax.rsqrt(mean_square + 1e-6)).astype(BF16)

    def exchange(source, dest, send_sem, recv_sem):
        def copy(peer, slot):
            return pltpu.make_async_remote_copy(
                src_ref=source.at[peer],
                dst_ref=dest.at[slot],
                send_sem=send_sem.at[peer],
                recv_sem=recv_sem.at[slot],
                device_id={"seq": peer},
                device_id_type=MESH,
            )

        return copy

    k_copy = exchange(k_send, k_recv, ksend_sem, krecv_sem)
    qv_copy = exchange(qv_send, qv_recv, qvsend_sem, qvrecv_sem)
    o_copy = exchange(o_send, o_recv, osend_sem, orecv_sem)

    def project(weight, base):
        res = jnp.dot(normed, weight, preferred_element_type=F32)
        for u in range(D // 128):
            qkv_t[pl.ds(base + u * 128, 128), :] = res[:, u * 128:(u + 1) * 128].T

    def head_rows(base, h):
        return qkv_t[pl.ds(base + h * HD, HD), :]

    def send_k(k, carry):
        k_copy(lax.rem(me + k, NS), me).start()
        return carry

    def send_qv(k, carry):
        qv_copy(lax.rem(me + NS - k, NS), me).start()
        return carry

    project(wqk_v[:, D:2 * D], 0)
    for h in range(H):
        k_send[h] = head_rows(0, h).astype(BF16)
    lax.fori_loop(1, NS, send_k, 0)
    k_recv[me] = k_send[me]
    project(wqk_v[:, 0:D], 0)
    project(wv_v[...], D)
    for h in range(H):
        qv_send[h] = jnp.concatenate([head_rows(0, h), head_rows(D, h)], axis=0).astype(BF16)
    lax.fori_loop(1, NS, send_qv, 0)
    qv_recv[me] = qv_send[me]

    row = bias_ref[pl.ds(me, 1), :] * LOG2E
    lane = lax.broadcasted_iota(jnp.int32, (NB, NB * NB), 1)
    sub = lax.broadcasted_iota(jnp.int32, (NB, NB * NB), 0)
    spread = jnp.where((lane & (NB - 1)) == sub, jnp.broadcast_to(row, (NB, NB * NB)), 0.0)
    top = spread.astype(BF16)
    left = spread - top.astype(F32)
    mid = left.astype(BF16)
    low = (left - mid.astype(F32)).astype(BF16)
    bias_rows = jnp.concatenate([top, mid, low], axis=0)
    row_bucket = (lax.broadcasted_iota(jnp.int32, (NB * NB, ROWS), 0) >> 4).astype(F32)
    row_index = lax.broadcasted_iota(jnp.int32, (NB, ROWS), 0).astype(F32)
    pad = jnp.zeros((32, ROWS), F32)

    def prepare_k(s):
        k = k_recv[s].astype(F32)
        onehot = (jnp.broadcast_to(b_recv[s].astype(F32), (NB, ROWS)) == row_index).astype(F32)
        off = pl.multiple_of(s * ROWS, ROWS)
        k_rows = jnp.concatenate([k, k, onehot, onehot, onehot, pad], axis=0)
        kaug[pl.ds(off, ROWS), :] = k_rows.T.astype(BF16)

    def take_k(k, carry):
        slot = lax.rem(me + NS - k, NS)
        b_copy(slot, slot).wait_recv()
        k_copy(slot, slot).wait_recv()
        prepare_k(slot)
        return carry

    prepare_k(me)
    lax.fori_loop(1, NS, take_k, 0)

    nq = NODES_G // QB
    per = QB // ROWS
    start = me // per

    def owner_of(i, u):
        return lax.rem(start + i, nq) * per + u

    def wait_q(i):
        for u in range(per):
            slot = owner_of(i, u)

            @pl.when((slot != me) & (i < nq))
            def _():
                qv_copy(slot, slot).wait_recv()

    def prepare_q(i):
        for u in range(per):
            slot = owner_of(i, u)
            q = qv_recv[slot].astype(F32)[0:HD] * SCALE_LOG2
            b = b_recv[slot].astype(F32)
            q_top = q.astype(BF16).astype(F32)
            chosen = (jnp.broadcast_to(b, (NB * NB, ROWS)) == row_bucket).astype(F32)
            q_bias = jnp.dot(bias_rows, chosen.astype(BF16), preferred_element_type=F32)
            q_all[i, :, u * ROWS:(u + 1) * ROWS] = jnp.concatenate(
                [q_top, q - q_top, q_bias, pad], axis=0
            ).astype(BF16)

    def place_v(i):
        for u in range(per):
            slot = owner_of(i, u)
            off = pl.multiple_of(slot * ROWS, ROWS)
            vaug_t[0:HD, pl.ds(off, ROWS)] = qv_recv[slot].astype(F32)[HD:2 * HD].astype(BF16)

    low_peak = jnp.full((8, QB), -3e38, F32)

    def scores(i, j, slot, peak):
        s = jnp.dot(kaug[pl.ds(j * KC, KC), :], q_all[i], preferred_element_type=F32)
        s_all[slot, pl.ds(j * KC, KC), :] = s
        return jnp.maximum(peak, jnp.max(s.reshape(KC // 8, 8, QB), axis=0))

    def early(i, carry):
        wait_q(i + 1)
        peak = low_peak
        for j in range(NODES_G // KC):
            peak = scores(i, j, i, peak)
        prepare_q(i + 1)
        place_v(i + 1)
        peaks[i] = peak
        return carry

    def step(i, slot, after):
        peak = jnp.max(peaks[i], axis=0, keepdims=True) - 2.0
        peak_out = low_peak
        acc = jnp.zeros((32, QB), F32)
        for j in range(NODES_G // KC):
            p = jnp.exp2((s_all[slot, pl.ds(j * KC, KC), :] - peak).astype(BF16))
            acc = acc + jnp.dot(
                vaug_t[:, pl.ds(j * KC, KC)], p, preferred_element_type=F32
            )
            if after:
                peak_out = scores(i + HELD, j, slot, peak_out)
        if after:
            prepare_q(i + HELD + 1)
            peaks[i + HELD] = peak_out
        res = (acc[0:HD] / acc[HD:HD + 1]).astype(BF16)
        for u in range(per):
            o_send[owner_of(i, u)] = res[:, u * ROWS:(u + 1) * ROWS]
        for u in range(per):
            owner = owner_of(i, u)

            @pl.when(owner != me)
            def _():
                o_copy(owner, me).start()

    def with_scores(i, carry):
        step(i, i, True)
        return carry

    def without_scores(i, carry):
        step(i, i - HELD, False)
        return carry

    def take_rest(i, carry):
        wait_q(i)
        place_v(i)
        return carry

    vaug_t[...] = jnp.ones((32, NODES_G), BF16)
    wait_q(0)
    prepare_q(0)
    place_v(0)
    lax.fori_loop(0, HELD, early, 0)
    lax.fori_loop(HELD + 1, nq, take_rest, 0)
    lax.fori_loop(0, nq - HELD, with_scores, 0)
    lax.fori_loop(nq - HELD, nq, without_scores, 0)
    o_recv[me] = o_send[me]

    def take_out(k, carry):
        slot = lax.rem(me + NS - k, NS)
        o_copy(slot, slot).wait_recv()
        return carry

    lax.fori_loop(1, NS, take_out, 0)
    for h in range(H):
        qkv_t[pl.ds(h * HD, HD), :] = o_recv[h].astype(F32)
    for u in range(D // 128):
        out_ref[:, u * 128:(u + 1) * 128] = qkv_t[pl.ds(u * 128, 128), :].T.astype(BF16)

    def drain(k, carry):
        peer = lax.rem(me + k, NS)
        for copy in (b_copy, k_copy, qv_copy, o_copy):
            copy(peer, me).wait_send()
        return carry

    lax.fori_loop(1, NS, drain, 0)
    for copy in sent:
        copy.wait_send()


def on_device(features, tiles, tile_src, tile_count, node_bucket, w_qk, w_v, bias_table):
    hbm = pl.BlockSpec(memory_space=pl.ANY)
    vmem = pl.BlockSpec(memory_space=pltpu.VMEM)
    smem = pl.BlockSpec(memory_space=pltpu.SMEM)
    dma = pltpu.SemaphoreType.DMA
    return pl.pallas_call(
        layer_kernel,
        out_shape=jax.ShapeDtypeStruct((ROWS, D), BF16),
        in_specs=[hbm, hbm, smem, smem, vmem, hbm, hbm, vmem],
        out_specs=vmem,
        scratch_shapes=[
            pltpu.VMEM((NG, ROWS, D), BF16),
            pltpu.VMEM((ROWS, TILES * ROWS), BF16),
            pltpu.VMEM((D, 2 * D), BF16),
            pltpu.VMEM((D, D), BF16),
            pltpu.VMEM((2 * D, ROWS), F32),
            pltpu.VMEM((NS, 1, ROWS), jnp.int32),
            pltpu.VMEM((NS, HD, ROWS), BF16),
            pltpu.VMEM((NS, HD, ROWS), BF16),
            pltpu.VMEM((NS, 2 * HD, ROWS), BF16),
            pltpu.VMEM((NS, 2 * HD, ROWS), BF16),
            pltpu.VMEM((NS, HD, ROWS), BF16),
            pltpu.VMEM((NS, HD, ROWS), BF16),
            pltpu.VMEM((NODES_G, 128), BF16),
            pltpu.VMEM((32, NODES_G), BF16),
            pltpu.VMEM((NODES_G // QB + 1, 128, QB), BF16),
            pltpu.VMEM((HELD, NODES_G, QB), F32),
            pltpu.VMEM((NODES_G // QB, 8, QB), F32),
            dma((15 * CHUNKS,)),
            dma((NG, CHUNKS)),
            dma((4,)),
        ] + [dma((NS,)) for _ in range(8)],
        compiler_params=pltpu.CompilerParams(
            collective_id=0, has_side_effects=True, vmem_limit_bytes=62 * 1024 * 1024
        ),
        name="layer",
    )(features, tiles, tile_src, tile_count, node_bucket.reshape(1, ROWS), w_qk, w_v, bias_table)


def solution(mesh):
    rows = P(("group", "seq"), None)
    line = P(("group", "seq"))
    return jax.shard_map(
        on_device,
        mesh=mesh,
        in_specs=(rows, rows, rows, line, line, P(), P(), P()),
        out_specs=rows,
        check_vma=False,
    )
```

```python
import functools
import math

import jax
import jax.numpy as jnp
from jax import lax
from jax.experimental import pallas as pl
from jax.experimental.pallas import tpu as pltpu
from jax.sharding import PartitionSpec as P

D = 768
H = 32
HD = 24
NB = 16
TILES = 8
ROWS = 128
NG = 16
NS = 32
NODES_G = ROWS * NS
HELD = 8
CHUNKS = 4
CROWS = ROWS // CHUNKS
QB = 256
KC = 1024
SCALE_LOG2 = math.log2(math.e) / math.sqrt(HD)
LOG2E = math.log2(math.e)
MESH = pl.DeviceIdType.MESH
F32 = jnp.float32
BF16 = jnp.bfloat16


def layer_kernel(
    x_ref, tiles_ref, src_ref, cnt_ref, bucket_ref, wqk_ref, wv_ref, bias_ref,
    out_ref,
    gath, tiles_v, wqk_v, wv_v, qkv_t,
    b_recv, k_send, k_recv, qv_send, qv_recv, o_send, o_recv,
    kaug, vaug_t, q_all, s_all, peaks,
    gsend_sem, grecv_sem, local_sem, bsend_sem, brecv_sem,
    ksend_sem, krecv_sem, qvsend_sem, qvrecv_sem, osend_sem, orecv_sem,
):
    g = lax.axis_index("group")
    me = lax.axis_index("seq")
    y = g // 4
    z = lax.rem(g, 4)

    def gid(yy, zz):
        return lax.rem(yy, 4) * 4 + lax.rem(zz, 4)

    zp, zm = gid(y, z + 1), gid(y, z + 3)
    yp, ym = gid(y + 1, z), gid(y + 3, z)

    barrier = pltpu.get_barrier_semaphore()
    for peer in (zp, zm, yp, ym):
        pl.semaphore_signal(barrier, inc=1, device_id={"group": peer}, device_id_type=MESH)

    def greet(k, carry):
        peer = lax.rem(me + k, NS)
        pl.semaphore_signal(barrier, inc=1, device_id={"seq": peer}, device_id_type=MESH)
        return carry

    lax.fori_loop(1, NS, greet, 0)

    own = pltpu.make_async_copy(x_ref, gath.at[g], local_sem.at[0])
    own.start()
    loads = [
        pltpu.make_async_copy(tiles_ref, tiles_v, local_sem.at[1]),
        pltpu.make_async_copy(wqk_ref, wqk_v, local_sem.at[2]),
        pltpu.make_async_copy(wv_ref, wv_v, local_sem.at[3]),
    ]
    for load in loads:
        load.start()
    pl.semaphore_wait(barrier, 4 + NS - 1)

    sent = []

    def block(origin, c):
        return gath.at[origin, pl.ds(c * CROWS, CROWS), :]

    def send(source, origin, c, peer):
        copy = pltpu.make_async_remote_copy(
            src_ref=source,
            dst_ref=block(origin, c),
            send_sem=gsend_sem.at[len(sent)],
            recv_sem=grecv_sem.at[origin, c],
            device_id={"group": peer},
            device_id_type=MESH,
        )
        copy.start()
        sent.append(copy)

    def first(c, peer):
        send(x_ref.at[pl.ds(c * CROWS, CROWS), :], g, c, peer)

    def forward(origin, c, peer):
        send(block(origin, c), origin, c, peer)

    arrived = set()

    def arrive(dy, dz, c):
        arrived.add((dy, dz, c))
        origin = gid(y + dy, z + dz)
        pltpu.make_async_remote_copy(
            src_ref=block(origin, c),
            dst_ref=block(origin, c),
            send_sem=gsend_sem.at[0],
            recv_sem=grecv_sem.at[origin, c],
            device_id={"group": zp},
            device_id_type=MESH,
        ).wait_recv()

    half = CHUNKS // 2
    upper = list(range(half))
    lower = list(range(CHUNKS - 1, half - 1, -1))
    pending = []

    def across(dz, c):
        forward(gid(y, z + dz), c, yp)
        forward(gid(y, z + dz), c, ym)
        pending.append((dz, c))

    def catch_up(keep):
        while len(pending) > keep:
            dz, c = pending.pop(0)
            dy, peer = (3, yp) if c < half else (1, ym)
            arrive(dy, dz, c)
            forward(gid(y + dy, z + dz), c, peer)

    for t, b in zip(upper, lower):
        first(b, zp)
        first(t, zm)
    for t, b in zip(upper, lower):
        first(t, zp)
        first(b, zm)
    for t, b in zip(upper, lower):
        for c in (t, b):
            first(c, yp)
            first(c, ym)
            pending.append((0, c))

    def b_copy(peer, slot):
        return pltpu.make_async_remote_copy(
            src_ref=bucket_ref,
            dst_ref=b_recv.at[slot],
            send_sem=bsend_sem.at[peer],
            recv_sem=brecv_sem.at[slot],
            device_id={"seq": peer},
            device_id_type=MESH,
        )

    def send_bucket(k, carry):
        b_copy(lax.rem(me + k, NS), me).start()
        return carry

    lax.fori_loop(1, NS, send_bucket, 0)
    b_recv[me] = bucket_ref[...]
    for t, b in zip(upper, lower):
        arrive(0, 3, b)
        across(3, b)
        arrive(0, 1, t)
        across(1, t)
        catch_up(4)
    for t, b in zip(upper, lower):
        arrive(0, 3, t)
        forward(zm, t, zp)
        arrive(0, 1, b)
        forward(zp, b, zm)
        across(3, t)
        across(1, b)
        catch_up(4)
    for t, b in zip(upper, lower):
        arrive(0, 2, t)
        across(2, t)
        arrive(0, 2, b)
        across(2, b)
        catch_up(4)
    catch_up(0)
    own.wait()
    for load in loads:
        load.wait()
    for dz in (0, 1, 3, 2):
        for dy in (1, 3, 2):
            for c in range(CHUNKS):
                if (dy, dz, c) not in arrived:
                    arrive(dy, dz, c)

    total = gath[g].astype(F32)
    count = cnt_ref[0]
    for t in range(TILES):
        live = jnp.where(t < count, 1.0, 0.0)
        chosen = gath[src_ref[0, t]]
        part = jnp.dot(
            tiles_v[:, t * ROWS:(t + 1) * ROWS], chosen, preferred_element_type=F32
        )
        total = total + part * live
    mean_square = jnp.mean(total * total, axis=-1, keepdims=True)
    normed = (total * lax.rsqrt(mean_square + 1e-6)).astype(BF16)

    def exchange(source, dest, send_sem, recv_sem):
        def copy(peer, slot):
            return pltpu.make_async_remote_copy(
                src_ref=source.at[peer],
                dst_ref=dest.at[slot],
                send_sem=send_sem.at[peer],
                recv_sem=recv_sem.at[slot],
                device_id={"seq": peer},
                device_id_type=MESH,
            )

        return copy

    k_copy = exchange(k_send, k_recv, ksend_sem, krecv_sem)
    qv_copy = exchange(qv_send, qv_recv, qvsend_sem, qvrecv_sem)
    o_copy = exchange(o_send, o_recv, osend_sem, orecv_sem)

    def project(weight, base):
        res = jnp.dot(normed, weight, preferred_element_type=F32)
        for u in range(D // 128):
            qkv_t[pl.ds(base + u * 128, 128), :] = res[:, u * 128:(u + 1) * 128].T

    def head_rows(base, h):
        return qkv_t[pl.ds(base + h * HD, HD), :]

    def send_k(k, carry):
        k_copy(lax.rem(me + k, NS), me).start()
        return carry

    def send_qv(k, carry):
        qv_copy(lax.rem(me + NS - k, NS), me).start()
        return carry

    project(wqk_v[:, D:2 * D], 0)
    for h in range(H):
        k_send[h] = head_rows(0, h).astype(BF16)
    lax.fori_loop(1, NS, send_k, 0)
    k_recv[me] = k_send[me]
    project(wqk_v[:, 0:D], 0)
    project(wv_v[...], D)
    for h in range(H):
        qv_send[h] = jnp.concatenate([head_rows(0, h), head_rows(D, h)], axis=0).astype(BF16)
    lax.fori_loop(1, NS, send_qv, 0)
    qv_recv[me] = qv_send[me]

    row = bias_ref[pl.ds(me, 1), :] * LOG2E
    lane = lax.broadcasted_iota(jnp.int32, (NB, NB * NB), 1)
    sub = lax.broadcasted_iota(jnp.int32, (NB, NB * NB), 0)
    spread = jnp.where((lane & (NB - 1)) == sub, jnp.broadcast_to(row, (NB, NB * NB)), 0.0)
    top = spread.astype(BF16)
    left = spread - top.astype(F32)
    mid = left.astype(BF16)
    low = (left - mid.astype(F32)).astype(BF16)
    bias_rows = jnp.concatenate([top, mid, low], axis=0)
    row_bucket = (lax.broadcasted_iota(jnp.int32, (NB * NB, ROWS), 0) >> 4).astype(F32)
    row_index = lax.broadcasted_iota(jnp.int32, (NB, ROWS), 0).astype(F32)
    pad = jnp.zeros((32, ROWS), F32)

    def prepare_k(s):
        k = k_recv[s].astype(F32)
        onehot = (jnp.broadcast_to(b_recv[s].astype(F32), (NB, ROWS)) == row_index).astype(F32)
        off = pl.multiple_of(s * ROWS, ROWS)
        k_rows = jnp.concatenate([k, k, onehot, onehot, onehot, pad], axis=0)
        kaug[pl.ds(off, ROWS), :] = k_rows.T.astype(BF16)

    def take_k(k, carry):
        slot = lax.rem(me + NS - k, NS)
        b_copy(slot, slot).wait_recv()
        k_copy(slot, slot).wait_recv()
        prepare_k(slot)
        return carry

    prepare_k(me)
    lax.fori_loop(1, NS, take_k, 0)

    nq = NODES_G // QB
    per = QB // ROWS
    start = me // per

    def owner_of(i, u):
        return lax.rem(start + i, nq) * per + u

    def wait_q(i):
        for u in range(per):
            slot = owner_of(i, u)

            @pl.when((slot != me) & (i < nq))
            def _():
                qv_copy(slot, slot).wait_recv()

    def prepare_q(i):
        for u in range(per):
            slot = owner_of(i, u)
            q = qv_recv[slot].astype(F32)[0:HD] * SCALE_LOG2
            b = b_recv[slot].astype(F32)
            q_top = q.astype(BF16).astype(F32)
            chosen = (jnp.broadcast_to(b, (NB * NB, ROWS)) == row_bucket).astype(F32)
            q_bias = jnp.dot(bias_rows, chosen.astype(BF16), preferred_element_type=F32)
            q_all[i, :, u * ROWS:(u + 1) * ROWS] = jnp.concatenate(
                [q_top, q - q_top, q_bias, pad], axis=0
            ).astype(BF16)

    def place_v(i):
        for u in range(per):
            slot = owner_of(i, u)
            off = pl.multiple_of(slot * ROWS, ROWS)
            vaug_t[0:HD, pl.ds(off, ROWS)] = qv_recv[slot].astype(F32)[HD:2 * HD].astype(BF16)

    low_peak = jnp.full((8, QB), -3e38, F32)

    def scores(i, j, slot, peak):
        s = jnp.dot(kaug[pl.ds(j * KC, KC), :], q_all[i], preferred_element_type=F32)
        s_all[slot, pl.ds(j * KC, KC), :] = s
        return jnp.maximum(peak, jnp.max(s.reshape(KC // 8, 8, QB), axis=0))

    def early(i, carry):
        wait_q(i + 1)
        peak = low_peak
        for j in range(NODES_G // KC):
            peak = scores(i, j, i, peak)
        prepare_q(i + 1)
        place_v(i + 1)
        peaks[i] = peak
        return carry

    def step(i, slot, after):
        peak = jnp.max(peaks[i], axis=0, keepdims=True) - 2.0
        peak_out = low_peak
        acc = jnp.zeros((32, QB), F32)
        for j in range(NODES_G // KC):
            p = jnp.exp2((s_all[slot, pl.ds(j * KC, KC), :] - peak).astype(BF16))
            acc = acc + jnp.dot(
                vaug_t[:, pl.ds(j * KC, KC)], p, preferred_element_type=F32
            )
            if after:
                peak_out = scores(i + HELD, j, slot, peak_out)
        if after:
            prepare_q(i + HELD + 1)
            peaks[i + HELD] = peak_out
        res = (acc[0:HD] / acc[HD:HD + 1]).astype(BF16)
        for u in range(per):
            o_send[owner_of(i, u)] = res[:, u * ROWS:(u + 1) * ROWS]
        for u in range(per):
            owner = owner_of(i, u)

            @pl.when(owner != me)
            def _():
                o_copy(owner, me).start()

    def with_scores(i, carry):
        step(i, i, True)
        return carry

    def without_scores(i, carry):
        step(i, i - HELD, False)
        return carry

    def take_rest(i, carry):
        wait_q(i)
        place_v(i)
        return carry

    vaug_t[...] = jnp.ones((32, NODES_G), BF16)
    wait_q(0)
    prepare_q(0)
    place_v(0)
    lax.fori_loop(0, HELD, early, 0)
    lax.fori_loop(HELD + 1, nq, take_rest, 0)
    lax.fori_loop(0, nq - HELD, with_scores, 0)
    lax.fori_loop(nq - HELD, nq, without_scores, 0)
    o_recv[me] = o_send[me]

    def take_out(k, carry):
        slot = lax.rem(me + NS - k, NS)
        o_copy(slot, slot).wait_recv()
        return carry

    lax.fori_loop(1, NS, take_out, 0)
    for h in range(H):
        qkv_t[pl.ds(h * HD, HD), :] = o_recv[h].astype(F32)
    for u in range(D // 128):
        out_ref[:, u * 128:(u + 1) * 128] = qkv_t[pl.ds(u * 128, 128), :].T.astype(BF16)

    def drain(k, carry):
        peer = lax.rem(me + k, NS)
        for copy in (b_copy, k_copy, qv_copy, o_copy):
            copy(peer, me).wait_send()
        return carry

    lax.fori_loop(1, NS, drain, 0)
    for copy in sent:
        copy.wait_send()


def on_device(features, tiles, tile_src, tile_count, node_bucket, w_qk, w_v, bias_table):
    hbm = pl.BlockSpec(memory_space=pl.ANY)
    vmem = pl.BlockSpec(memory_space=pltpu.VMEM)
    smem = pl.BlockSpec(memory_space=pltpu.SMEM)
    dma = pltpu.SemaphoreType.DMA
    return pl.pallas_call(
        layer_kernel,
        out_shape=jax.ShapeDtypeStruct((ROWS, D), BF16),
        in_specs=[hbm, hbm, smem, smem, vmem, hbm, hbm, vmem],
        out_specs=vmem,
        scratch_shapes=[
            pltpu.VMEM((NG, ROWS, D), BF16),
            pltpu.VMEM((ROWS, TILES * ROWS), BF16),
            pltpu.VMEM((D, 2 * D), BF16),
            pltpu.VMEM((D, D), BF16),
            pltpu.VMEM((2 * D, ROWS), F32),
            pltpu.VMEM((NS, 1, ROWS), jnp.int32),
            pltpu.VMEM((NS, HD, ROWS), BF16),
            pltpu.VMEM((NS, HD, ROWS), BF16),
            pltpu.VMEM((NS, 2 * HD, ROWS), BF16),
            pltpu.VMEM((NS, 2 * HD, ROWS), BF16),
            pltpu.VMEM((NS, HD, ROWS), BF16),
            pltpu.VMEM((NS, HD, ROWS), BF16),
            pltpu.VMEM((NODES_G, 128), BF16),
            pltpu.VMEM((32, NODES_G), BF16),
            pltpu.VMEM((NODES_G // QB + 1, 128, QB), BF16),
            pltpu.VMEM((HELD, NODES_G, QB), F32),
            pltpu.VMEM((NODES_G // QB, 8, QB), F32),
            dma((15 * CHUNKS,)),
            dma((NG, CHUNKS)),
            dma((4,)),
        ] + [dma((NS,)) for _ in range(8)],
        compiler_params=pltpu.CompilerParams(
            collective_id=0, has_side_effects=True, vmem_limit_bytes=62 * 1024 * 1024
        ),
        name="layer",
    )(features, tiles, tile_src, tile_count, node_bucket.reshape(1, ROWS), w_qk, w_v, bias_table)


def solution(mesh):
    rows = P(("group", "seq"), None)
    line = P(("group", "seq"))
    return jax.shard_map(
        on_device,
        mesh=mesh,
        in_specs=(rows, rows, rows, line, line, P(), P(), P()),
        out_specs=rows,
        check_vma=False,
    )
```
